32 devices in a mesh: group: 4 (over z), local: 8 (over y, x, core).
Axes of the slice: x: 2, y: 2, z: 4, core: 2. Of those that a mesh axis runs over, the one named last changes fastest.
Arguments:
- tokens: bfloat16 [4096, 4096], P(('group', 'local')), may hold values from -6 to 6
- expert_ids: int32 [4096, 8], P(('group', 'local')), may hold values from 0 to 31, all different within a row; in each aligned block of 128 rows (0 to 127, 128 to 255, ...) at most 40 rows name the same one
- combine: float32 [4096, 8], P(('group', 'local')), may hold values from 0.02 to 0.5
- gate_w: bfloat16 [32, 4096, 768], P(('group', 'local')), may hold values from -0.09375 to 0.09375
- up_w: bfloat16 [32, 4096, 768], P(('group', 'local')), may hold values from -0.09375 to 0.09375
- down_w: bfloat16 [32, 768, 4096], P(('group', 'local')), may hold values from -0.21875 to 0.21875
Outputs:
- mixed: bfloat16 [4096, 4096], P(('group', 'local'))
The draws below stay inside these ranges and needn't reach their ends.
Inputs may be any that keep to these rules, and one draw needn't show every extreme that they name: `expert_ids`: each token names 8 different experts; among the 128 tokens of one device (aligned blocks) no expert is named more than 40 times, a bound that some block reaches.
All inputs are finite; a program needn't handle non-finite values.
Results may differ from the reference program's by a relative error of at most 0.0057.
Values may be sent and summed in bfloat16 or wider, within the bound.
A program may use at most 128 MiB of HBM per device.

```python
import math
import jax
import jax.numpy as jnp
import numpy as np
from jax import lax

D = 4096
FF = 768
TOP = 8
TOK_DEV = 128
EXPERTS = 32
CAP = 40
TOKENS = 4096
N_GROUP = 4
N_LOCAL = 8


def steps_of(rng, dims, shards, low, high):
    level = 1.0
    for dim, shards_of in shards:
        steps = jax.random.uniform(jax.random.fold_in(jax.random.fold_in(rng, 6), dim), (shards_of,), jnp.float32, low / len(shards), high / len(shards))
        level = level * jnp.repeat(jnp.exp(steps), dims[dim] // shards_of).reshape((-1,) + (1,) * (len(dims) - 1 - dim))
    return level


def deal_out(own_key, own, number, rows, count, top, bound, slope):
    order = jax.random.permutation(own_key, count)
    heavy_load, ordinary = load_shares(count, rows * top, bound, slope, True), load_shares(count, rows * top, bound, slope, False)
    places = jnp.arange(count)

    def named(sizes, offset_by):
        used = int((sizes > 0).sum())
        fixed = max(1, used // 4)
        passed = fixed + (places - fixed + offset_by * (used - fixed)) % max(1, count - fixed)
        return jnp.zeros((count,), jnp.int32).at[order[jnp.where(places < fixed, places, passed)]].set(jnp.asarray(sizes, jnp.int32))

    sizes = jnp.where(number % 4 == 0, named(heavy_load, number // 4), named(ordinary, number - number // 4 - 1))
    mixed = jax.random.permutation(jax.random.fold_in(own, 3), count)
    giver, taker = mixed[0:count // 2 * 2:2], mixed[1:count // 2 * 2:2]
    room = jnp.minimum(sizes[giver] - 1, bound - sizes[taker]) // 2
    room = jnp.where((giver == order[0]) | (taker == order[0]) | (sizes[taker] == 0), 0, jnp.maximum(room, 0))
    passed = jax.random.randint(jax.random.fold_in(own, 4), (count // 2,), 0, 1 << 20) % (room + 1)
    sizes = sizes.at[giver].add(-passed).at[taker].add(passed)
    labels = jnp.searchsorted(jnp.cumsum(sizes), jnp.arange(rows * top), side="right").astype(jnp.int32)
    listing = labels.reshape(top, rows).T
    listing = listing[jax.random.permutation(jax.random.fold_in(own, 1), rows)]
    offset_by = jax.random.randint(jax.random.fold_in(own, 2), (rows, 1), 0, top)
    return jnp.take_along_axis(listing, (jnp.arange(top)[None, :] + offset_by) % top, axis=1)


def load_shares(amount, total, most, lean, full):
    loads = [(1 << 20) // math.isqrt(rank ** lean) + 1 for rank in range(1, amount + 1)]
    largest = most if full else min(most, max(-(-total // amount), total * loads[0] // sum(loads)))
    least = 1 if total - largest >= amount - 1 else 0
    given, rest = [largest] + [least] * (amount - 1), total - largest - least * (amount - 1)
    while rest > 0:
        free = [i for i in range(1, amount) if given[i] < largest] or [i for i in range(1, amount) if given[i] < most]
        pool, budget = sum([loads[i] for i in free]), rest
        for i in free:
            more = min(most - given[i], max(1, budget * loads[i] // pool), rest)
            given[i] = given[i] + more
            rest = rest - more
    return np.array(given)


def normal_values(stream_key, dims, spread, bound, cuts=(), kind=jnp.bfloat16):
    loudness = steps_of(stream_key, dims, cuts, -0.22, 0.18) if cuts else 1.0
    values = jax.random.normal(stream_key, dims, jnp.float32) * spread * loudness
    return jnp.minimum(jnp.maximum(values, -bound), bound).astype(kind)


def setup_inputs(seed: int = 0) -> dict:
    streams_of = jax.random.split(jax.random.key(seed), 7)
    tokens = normal_values(streams_of[0], (TOKENS, D), 1.0, 6.0, ((0, 32),))
    expert_ids_keys = jax.random.split(jax.random.fold_in(streams_of[1], 1), TOKENS // TOK_DEV)
    expert_ids_turns = jax.random.permutation(jax.random.fold_in(streams_of[1], 3), TOKENS // TOK_DEV)
    expert_ids = jax.vmap(lambda own, number: deal_out(jax.random.fold_in(streams_of[1], 2), own, number, TOK_DEV, EXPERTS, TOP, CAP, 1))(expert_ids_keys, expert_ids_turns).reshape((TOKENS, TOP))
    combine = jnp.clip(jnp.exp(math.log(0.5) - 3.218876 * jax.random.uniform(streams_of[2], (TOKENS, TOP), jnp.float32) ** steps_of(streams_of[2], (TOKENS, TOP), ((0, 32),), -0.2, 0.2)), 0.02, 0.5)
    gate_w = normal_values(streams_of[3], (EXPERTS, D, FF), D ** -0.5, 0.09375, ((0, 32),))
    up_w = normal_values(streams_of[4], (EXPERTS, D, FF), D ** -0.5, 0.09375, ((0, 32),))
    down_w = normal_values(streams_of[5], (EXPERTS, FF, D), FF ** -0.5, 0.21875, ((0, 32),))
    return {"tokens": tokens, "expert_ids": expert_ids, "combine": combine, "gate_w": gate_w, "up_w": up_w, "down_w": down_w}


def reference(tokens, expert_ids, combine, gate_w, up_w, down_w):
    devices = N_GROUP * N_LOCAL
    flat_ids = expert_ids.reshape(devices, TOK_DEV * TOP).astype(jnp.int32)
    one_hot = (flat_ids[:, :, None] == jnp.arange(EXPERTS, dtype=jnp.int32)[None, None, :]).astype(jnp.int32)
    slot_index = jnp.sum((jnp.cumsum(one_hot, axis=1) - one_hot) * one_hot, axis=2).astype(jnp.int32)
    source = jnp.arange(devices, dtype=jnp.int32)[:, None]
    position = (flat_ids * (devices * CAP) + source * CAP + slot_index).reshape(-1)
    token_of = (jnp.arange(TOKENS * TOP, dtype=jnp.int32) // TOP).astype(jnp.int32)
    table = jnp.full((EXPERTS * devices * CAP,), TOKENS, jnp.int32).at[position].set(token_of)
    weight_table = jnp.zeros((EXPERTS * devices * CAP,), jnp.float32).at[position].set(combine.reshape(-1))
    padded = jnp.concatenate([tokens, jnp.zeros((1, D), tokens.dtype)], axis=0)

    def one_expert(total, inputs):
        gate_e, up_e, down_e, rows_e, weight_e = inputs
        chosen = padded[rows_e].astype(jnp.float32)
        gate_part = jnp.dot(chosen, gate_e.astype(jnp.float32), preferred_element_type=jnp.float32)
        up_part = jnp.dot(chosen, up_e.astype(jnp.float32), preferred_element_type=jnp.float32)
        hidden = (jax.nn.silu(gate_part) * up_part).astype(jnp.bfloat16)
        result = jnp.dot(hidden.astype(jnp.float32), down_e.astype(jnp.float32), preferred_element_type=jnp.float32).astype(jnp.bfloat16)
        total = total.at[rows_e].add(weight_e[:, None] * result.astype(jnp.float32))
        return total, None

    start = jnp.zeros((TOKENS + 1, D), jnp.float32)
    total, _ = lax.scan(one_expert, start, (gate_w, up_w, down_w, table.reshape(EXPERTS, devices * CAP), weight_table.reshape(EXPERTS, devices * CAP)))
    return total[:TOKENS].astype(jnp.bfloat16)
```

```python
import jax
import jax.numpy as jnp
from jax import lax
from jax.sharding import PartitionSpec as P


def routing(expert_ids, combine, experts):
    rows = expert_ids.shape[0]
    named = expert_ids.T[:, None, :] == jnp.arange(experts, dtype=jnp.int32)[None, :, None]
    member = jnp.sum(named.astype(jnp.float32), axis=0)
    weight = jnp.sum(jnp.where(named, combine.T[:, None, :], 0.0), axis=0)
    before = (jnp.arange(rows)[:, None] < jnp.arange(rows)[None, :]).astype(jnp.bfloat16)
    rank = jnp.dot(member.astype(jnp.bfloat16), before, preferred_element_type=jnp.float32)
    return jnp.where(member > 0, rank, -1.0), weight


def plain(tokens, expert_ids, combine, gate_w, up_w, down_w):
    rows, features = tokens.shape
    groups = lax.axis_size("group")
    members = lax.axis_size("local")
    experts = groups * members
    capacity = max(2, rows * expert_ids.shape[1] * 5 // (4 * experts))
    slot, weight = routing(expert_ids, combine, experts)
    table = jnp.stack([slot, weight]).reshape(2, groups, members, rows)
    table = lax.all_to_all(table, "group", split_axis=1, concat_axis=1, tiled=True)
    slot, weight = table[0], table[1]
    blocks = lax.all_gather(tokens, "group")
    picks = slot[:, :, None, :] == jnp.arange(capacity, dtype=jnp.float32)[None, None, :, None]
    chosen = jnp.einsum(
        "blct,btd->blcd", picks.astype(jnp.bfloat16), blocks, preferred_element_type=jnp.float32
    ).astype(jnp.bfloat16)
    arrived = lax.all_to_all(chosen, "local", split_axis=1, concat_axis=1, tiled=True)
    x = arrived.reshape(-1, features)
    gate_part = jnp.dot(x, gate_w[0], preferred_element_type=jnp.float32)
    up_part = jnp.dot(x, up_w[0], preferred_element_type=jnp.float32)
    hidden = (jax.nn.silu(gate_part) * up_part).astype(jnp.bfloat16)
    result = jnp.dot(hidden, down_w[0], preferred_element_type=jnp.float32).astype(jnp.bfloat16)
    returned = lax.all_to_all(
        result.reshape(arrived.shape), "local", split_axis=1, concat_axis=1, tiled=True
    ).reshape(groups, members * capacity, features)
    mix = jnp.where(picks, weight[:, :, None, :], 0.0).reshape(groups, members * capacity, rows)
    high = mix.astype(jnp.bfloat16)
    low = (mix - high.astype(jnp.float32)).astype(jnp.bfloat16)
    part = jnp.einsum("bct,bcd->btd", high, returned, preferred_element_type=jnp.float32)
    part = part + jnp.einsum("bct,bcd->btd", low, returned, preferred_element_type=jnp.float32)
    return lax.psum_scatter(part.astype(jnp.bfloat16), "group", scatter_dimension=0, tiled=False)


def solution(mesh):
    rows = P(("group", "local"), None)
    banks = P(("group", "local"), None, None)
    return jax.shard_map(
        plain,
        mesh=mesh,
        in_specs=(rows, rows, rows, banks, banks, banks),
        out_specs=rows,
        check_vma=False,
    )
```
